32 devices in a mesh: seq: 16 (over z, x, core), head: 2 (over y).
Axes of the slice: x: 2, y: 2, z: 4, core: 2. Of those that a mesh axis runs over, the one named last changes fastest.
Arguments:
- queries: bfloat16 [8192, 8192], P('seq', 'head'), may hold values from -6 to 6
- key_rows: bfloat16 [8192, 8192], P('seq', 'head'), may hold values from -6 to 6
- values: bfloat16 [8192, 8192], P('seq', 'head'), may hold values from -360 to 360
- slopes: float32 [64], P('head'), may hold values from 3.6621094e-05 to 0.06, as said below
- doc_lengths: int32 [8], replicated, may hold values from 1 to 4096, 8192 in all
- norm_gain: float32 [8192], P('head'), may hold values from 0.1 to 1.9
Outputs:
- attended: bfloat16 [8192, 8192], P('seq', 'head')
The draws below stay inside these ranges and needn't reach their ends.
Inputs may be any that keep to these rules, and one draw needn't show every extreme that they name: `slopes`: each head's rate lies between 0.3 / 8192 and 0.06.
All inputs are finite; a program needn't handle non-finite values.
Results may differ from the reference program's by a relative error of at most 0.0056.
Values may be sent and summed in bfloat16 or wider, within the bound.
A program may use at most 128 MiB of HBM per device.

```python
import math
import jax
import jax.numpy as jnp
import numpy as np
from jax import lax

H = 64
DH = 128
BLOCK = 256
DOCS = 8
TOKENS = 8192
MOST = 4096


def draw_slopes(key, part):
    key_slow, key_fast, key_pick = jax.random.split(key, 3)
    lowest = math.log(0.3 / TOKENS)
    middle = math.log(2.3 / TOKENS)
    highest = math.log(0.06)
    slow_rates = jnp.exp(jax.random.uniform(key_slow, (H,), jnp.float32, lowest, middle))
    fast_rates = jnp.exp(jax.random.uniform(key_fast, (H,), jnp.float32, middle, highest))
    share = 0.5
    picked = jax.random.uniform(key_pick, (H,), jnp.float32) < share
    return jnp.where(picked, slow_rates, fast_rates).astype(jnp.float32)


def draw_values(key, part):
    key_main, key_cols = jax.random.split(key, 2)
    columns = jnp.arange(H * DH, dtype=jnp.int32)
    head_place = (columns // DH).astype(jnp.float32) / max(H - 1, 1)
    base_draw = jnp.clip(jax.random.normal(key_main, (TOKENS, H * DH), jnp.float32), -4.0, 4.0)
    head_ramp = jnp.exp(math.log(3.0) * head_place)
    column_scale = jnp.exp(jax.random.uniform(key_cols, (H * DH,), jnp.float32, 0.0, math.log(10.0)))
    return (base_draw * (head_ramp * column_scale)[None, :]).astype(jnp.bfloat16)


def block_levels(key, extent, pieces, least, high):
    factor_of = 1.0
    for axis_at, shards_of in pieces:
        draws = jax.random.uniform(jax.random.fold_in(jax.random.fold_in(key, 6), axis_at), (shards_of,), jnp.float32, least / len(pieces), high / len(pieces))
        factor_of = factor_of * jnp.repeat(jnp.exp(draws), extent[axis_at] // shards_of).reshape((-1,) + (1,) * (len(extent) - 1 - axis_at))
    return factor_of


def split_up(number_of, total, bound, lean):
    weights = [(1 << 20) // math.isqrt(grade ** lean) + 1 for grade in range(2, number_of + 1)]
    spare, holding = total - bound - (number_of - 1), [1] * (number_of - 1)
    while spare > 0:
        movable = [i for i in range(number_of - 1) if holding[i] < bound]
        mass, budget = sum([weights[i] for i in movable]), spare
        for i in movable:
            more = min(bound - holding[i], max(1, budget * weights[i] // mass), spare)
            holding[i] = holding[i] + more
            spare = spare - more
    return np.array([bound] + holding)


def uneven_parts(stream_key, amount, total, bound, skew):
    if amount == 2:
        one = jax.random.randint(stream_key, (), max(1, total - bound), min(bound, total - 1) + 1)
        return jnp.stack([one, total - one])
    sizes = jnp.asarray(split_up(amount, total, bound, skew), jnp.int32)
    pairs = (amount - 1) // 2
    source_of, receiver = sizes[1:1 + 2 * pairs:2], sizes[2:2 + 2 * pairs:2]
    room = jnp.minimum(source_of - 1, bound - receiver)
    passed = jax.random.randint(jax.random.fold_in(stream_key, 1), (pairs,), 0, 1 << 20) % (room + 1)
    sizes = sizes.at[1:1 + 2 * pairs:2].set(source_of - passed).at[2:2 + 2 * pairs:2].set(receiver + passed)
    return sizes[jax.random.permutation(jax.random.fold_in(stream_key, 2), amount)]


def noise(key, extent, width, most, cuts=(), held_as=jnp.bfloat16):
    level = block_levels(key, extent, cuts, -0.22, 0.18) if cuts else 1.0
    values = jax.random.normal(key, extent, jnp.float32) * width * level
    return jnp.minimum(jnp.maximum(values, -most), most).astype(held_as)


def setup_inputs(seed: int = 0) -> dict:
    key_of = jax.random.split(jax.random.key(seed), 7)
    queries = noise(key_of[0], (TOKENS, H * DH), 1.0, 6.0, ((0, 16), (1, 2)))
    key_rows = noise(key_of[1], (TOKENS, H * DH), 1.0, 6.0, ((0, 16), (1, 2)))
    values = draw_values(jax.random.fold_in(key_of[6], 71), 0)
    slopes = draw_slopes(jax.random.fold_in(key_of[6], 71), 0)
    doc_lengths = uneven_parts(key_of[4], DOCS, TOKENS, MOST, 2).astype(jnp.int32)
    norm_gain = jnp.clip(1.0 + 0.18 * jax.random.normal(key_of[5], (H * DH,), jnp.float32), 0.1, 1.9)
    return {"queries": queries, "key_rows": key_rows, "values": values, "slopes": slopes, "doc_lengths": doc_lengths, "norm_gain": norm_gain}


def segment_of(positions, doc_lengths):
    starts = jnp.cumsum(doc_lengths) - doc_lengths
    later_starts = starts[1:]
    counted = lax.optimization_barrier(jnp.sum((positions[..., None] >= later_starts).astype(jnp.int32), axis=-1))
    return jnp.where(positions < 0, -1, counted).astype(jnp.int32)

def reference(queries, key_rows, values, slopes, doc_lengths, norm_gain):
    blocks = TOKENS // BLOCK
    query_all = queries.reshape(blocks, BLOCK, H, DH)
    key_all = key_rows.reshape(blocks, BLOCK, H, DH)
    value_all = values.reshape(blocks, BLOCK, H, DH)
    offsets = jnp.arange(BLOCK, dtype=jnp.int32)
    lags = offsets[:, None] - offsets[None, :]

    def advance(state, inputs):
        query_block, key_block, value_block, index = inputs
        first = index * BLOCK
        positions = first + offsets
        segment = segment_of(positions, doc_lengths)
        before = segment_of(first - 1 + jnp.zeros((1,), jnp.int32), doc_lengths)[0]
        query_wide = query_block.astype(jnp.float32)
        key_wide = key_block.astype(jnp.float32)
        value_wide = value_block.astype(jnp.float32)
        allowed = (lags >= 0) & (segment[:, None] == segment[None, :])
        distance = jnp.maximum(lags, 0).astype(jnp.float32)
        decay_mask = jnp.where(allowed[None], jnp.exp(-slopes[:, None, None] * distance[None]), 0.0)
        scores = jnp.einsum('thd,shd->hts', query_wide, key_wide)
        weights = lax.optimization_barrier((scores * decay_mask).astype(jnp.bfloat16)).astype(jnp.float32)
        intra_part = jnp.einsum('hts,shd->thd', weights, value_wide)
        remaining = (BLOCK - 1 - offsets).astype(jnp.float32)
        scale_rows = jnp.where((segment == segment[-1])[:, None], jnp.exp(-slopes[None, :] * remaining[:, None]), 0.0)
        weighted = lax.optimization_barrier((scale_rows[:, :, None] * value_wide).astype(jnp.bfloat16)).astype(jnp.float32)
        local_state = jnp.einsum('shd,she->hde', key_wide, weighted)
        factor = jnp.where(before == segment[-1], jnp.exp(-slopes * BLOCK), 0.0)
        entering = lax.optimization_barrier(state.astype(jnp.bfloat16)).astype(jnp.float32)
        reach = (offsets + 1).astype(jnp.float32)
        carry_rows = jnp.where((segment == before)[:, None], jnp.exp(-slopes[None, :] * reach[:, None]), 0.0)
        inter_part = jnp.einsum('thd,hde->the', query_wide, entering) * carry_rows[:, :, None]
        mixed = (intra_part + inter_part).reshape(BLOCK, H * DH)
        mean_square = lax.optimization_barrier(jnp.mean(mixed * mixed, axis=1, keepdims=True))
        result = (mixed * lax.rsqrt(mean_square + 1e-05) * norm_gain[None, :]).astype(jnp.bfloat16)
        return (factor[:, None, None] * state + local_state, result)
    initial = jnp.zeros((H, DH, DH), jnp.float32)
    _, results = lax.scan(advance, initial, (query_all, key_all, value_all, jnp.arange(blocks, dtype=jnp.int32)))
    return results.reshape(TOKENS, H * DH)
```

```python
import functools

import jax
import jax.numpy as jnp
from jax import lax
from jax.experimental import pallas as pl
from jax.experimental.pallas import tpu as pltpu
from jax.sharding import PartitionSpec as P

BLOCK = 256
FAR = 1e30
F32 = jnp.float32
BF16 = jnp.bfloat16
MESH = pl.DeviceIdType.MESH


def kernel(
    planes, head_parts, heads, blocks, parts,
    slopes_ref, docs_ref, q_hbm, k_hbm, v_hbm,
    mixed_hbm, inv_ref,
    q_ref, k_ref, v_ref, mixed_ref, out_ref, local_ref, own_ref, carry_ref,
    s_send, s_recv, p_send, p_recv, x_recv, c_send, c_recv,
    lag_ref, same_ref, tail_ref, lead_ref, rem_ref, reach_ref, sq_ref, sq_send, sq_recv,
    q_sem, k_sem, v_sem, o_sem,
    s_out, s_in, p_out, p_in, x_out, x_in, c_out, c_in, sq_out, sq_in,
):
    half = heads // 2
    step = half // parts
    chunks = 2 * parts
    rows = blocks * BLOCK
    size = q_ref.shape[1] // heads
    seq = lax.axis_index("seq")
    headpos = lax.axis_index("head")
    core = lax.rem(seq, 2)
    side = lax.rem(lax.div(seq, 2), 2)
    plane = lax.div(seq, 4)
    partner = seq + 1 - 2 * core
    across = seq + 2 - 4 * side
    ahead = jnp.minimum(seq + 4, 4 * planes - 1)
    first = (1 - core) * half

    def head_of(o):
        return lax.rem(o + first, heads)

    def cols(h):
        return pl.ds(pl.multiple_of(h * size, size), size)

    def wide(oc):
        return pl.ds(pl.multiple_of(head_of(oc * step) * size, step * size), step * size)

    def load(hbm, ref, sem, oc):
        return pltpu.make_async_copy(hbm.at[:, wide(oc)], ref.at[:, wide(oc)], sem.at[oc])

    def store(oc):
        return pltpu.make_async_copy(out_ref.at[:, wide(oc)], mixed_hbm.at[:, wide(oc)], o_sem.at[oc])

    def piece(c):
        return pl.ds(c * step, step)

    def remote(src, dst, c, out_sem, in_sem, target):
        return pltpu.make_async_remote_copy(
            src_ref=src.at[piece(c)], dst_ref=dst.at[piece(c)],
            send_sem=out_sem.at[c], recv_sem=in_sem.at[c],
            device_id={"seq": target}, device_id_type=MESH,
        )

    def s_copy(c):
        return remote(s_send, s_recv, c, s_out, s_in, partner)

    def p_copy(c):
        return remote(p_send, p_recv, c, p_out, p_in, ahead)

    def x_copy(c, src):
        return remote(src, x_recv, c, x_out, x_in, across)

    def c_copy(c):
        return remote(c_send, c_recv, c, c_out, c_in, partner)

    def each(count, body, start=0):
        def turn(i, _):
            body(i)
            return 0
        lax.fori_loop(start, count, turn, 0)

    barrier = pltpu.get_barrier_semaphore()
    pl.semaphore_signal(barrier, inc=1, device_id={"seq": partner}, device_id_type=MESH)
    pl.semaphore_signal(barrier, inc=1, device_id={"seq": across}, device_id_type=MESH)

    @pl.when(plane < planes - 1)
    def _():
        pl.semaphore_signal(barrier, inc=1, device_id={"seq": seq + 4}, device_id_type=MESH)

    @pl.when(plane > 0)
    def _():
        pl.semaphore_signal(barrier, inc=1, device_id={"seq": seq - 4}, device_id_type=MESH)

    for i in range(1, head_parts):
        pl.semaphore_signal(
            barrier, inc=1, device_id={"head": lax.rem(headpos + i, head_parts)}, device_id_type=MESH
        )

    def begin_kv(oc):
        load(k_hbm, k_ref, k_sem, oc).start()
        load(v_hbm, v_ref, v_sem, oc).start()

    each(chunks, begin_kv)
    each(chunks, lambda oc: load(q_hbm, q_ref, q_sem, oc).start())

    starts = []
    total = jnp.int32(0)
    for j in range(docs_ref.shape[0] - 1):
        total = total + docs_ref[j]
        starts.append(total)

    def segment(pos):
        counted = jnp.zeros_like(pos)
        for s in starts:
            counted = counted + jnp.where(pos >= s, 1, 0)
        return jnp.where(pos < 0, -1, counted)

    def joined(a, b):
        return jnp.where(segment(a) == segment(b), F32(1), F32(0))

    base = seq * rows
    chip = base - core * rows
    down = lax.broadcasted_iota(jnp.int32, (BLOCK, BLOCK), 0)
    along = lax.broadcasted_iota(jnp.int32, (BLOCK, BLOCK), 1)
    lag_ref[...] = jnp.where(down >= along, (down - along).astype(F32), F32(FAR))
    offs = lax.broadcasted_iota(jnp.int32, (BLOCK, size), 0)
    rem_ref[...] = (BLOCK - 1 - offs).astype(F32)
    reach_ref[...] = (offs + 1).astype(F32)
    within = []
    for b in range(blocks):
        b0 = base + b * BLOCK
        row_seg = segment(b0 + offs)
        same_ref[b] = jnp.where(segment(b0 + down) == segment(b0 + along), F32(1), F32(0))
        tail_ref[b] = jnp.where(row_seg == segment(b0 + BLOCK - 1), F32(1), F32(0))
        lead_ref[b] = jnp.where(row_seg == segment(b0 - 1), F32(1), F32(0))
        within.append(joined(b0 - 1, b0 + BLOCK - 1))
    j_cores = joined(chip + rows - 1, chip + 2 * rows - 1)
    j_first = joined(chip - 1, chip + rows - 1)
    j_chain = joined(chip - 2 * rows - 1, chip + 2 * rows - 1)
    j_skip = joined(chip - 2 * rows - 1, chip - 1)

    def fade(h, distance, keep):
        return jnp.exp(jnp.full((1, size), -slopes_ref[h] * distance, F32)) * keep

    sq_ref[...] = jnp.zeros_like(sq_ref)

    @pl.when(plane == 0)
    def _():
        p_recv[...] = jnp.zeros_like(p_recv)

    def end_state(h):
        r = slopes_ref[h]
        scale = jnp.exp(rem_ref[...] * (-r))
        state = None
        for b in range(blocks):
            here = pl.ds(b * BLOCK, BLOCK)
            weighted = (scale * tail_ref[b] * v_ref[here, cols(h)].astype(F32)).astype(BF16)
            one = lax.dot_general(
                k_ref[here, cols(h)], weighted, (((0,), (0,)), ((), ())), preferred_element_type=F32
            )
            if b < blocks - 1:
                local_ref[b, h] = one
            state = one if state is None else fade(h, F32(BLOCK), within[b]) * state + one
        return state

    def wait_kv(oc):
        load(k_hbm, k_ref, k_sem, oc).wait()
        load(v_hbm, v_ref, v_sem, oc).wait()

    def give(i):
        s_send[i] = end_state(first + i).astype(BF16)

    def keep(i):
        own_ref[i] = end_state(core * half + i)

    def first_chunk(c):
        wait_kv(c)
        each((c + 1) * step, give, c * step)

    first_chunk(jnp.int32(0))
    beside = jnp.where(plane > 0, 1, 0) + jnp.where(plane < planes - 1, 1, 0)
    pl.semaphore_wait(barrier, 1 + head_parts + beside)
    s_copy(0).start()

    def next_chunk(c):
        first_chunk(c)
        s_copy(c).start()

    each(parts, next_chunk, 1)

    def own_chunk(c):
        wait_kv(parts + c)
        each((c + 1) * step, keep, c * step)

    each(parts, own_chunk)

    def intra(h):
        decay = jnp.exp(lag_ref[...] * (-slopes_ref[h]))
        for b in range(blocks):
            here = pl.ds(b * BLOCK, BLOCK)
            scores = lax.dot_general(
                q_ref[here, cols(h)], k_ref[here, cols(h)], (((1,), (1,)), ((), ())),
                preferred_element_type=F32,
            )
            weights = (scores * decay * same_ref[b]).astype(BF16)
            mixed_ref[here, cols(h)] = jnp.dot(
                weights, v_ref[here, cols(h)], preferred_element_type=F32
            )

    def intra_chunk(oc):
        load(q_hbm, q_ref, q_sem, oc).wait()
        each((oc + 1) * step, lambda o: intra(head_of(o)), oc * step)

    is_second = core == 1

    def chip_states(i):
        mine, other = own_ref[i], s_recv[i].astype(F32)
        return jnp.where(is_second, other, mine), jnp.where(is_second, mine, other)

    def chain(i):
        h = core * half + i
        early, late = chip_states(i)
        chip_state = fade(h, F32(rows), j_cores) * early + late
        p_send[i] = (fade(h, F32(4 * rows), j_chain) * p_recv[i].astype(F32) + chip_state).astype(BF16)

    def chain_chunk(c):
        s_copy(c).wait_recv()

        @pl.when(plane > 0)
        def _():
            p_copy(c).wait_recv()

        @pl.when(side == 1)
        def _():
            x_copy(c, p_recv).start()

        each((c + 1) * step, chain, c * step)

        @pl.when(plane < planes - 1)
        def _():
            p_copy(c).start()

        @pl.when(side == 0)
        def _():
            x_copy(c, p_send).start()

    head_start = jnp.minimum(plane, parts)
    each(head_start, intra_chunk)

    def chain_and_intra(c):
        chain_chunk(c)
        intra_chunk(head_start + c)

    each(parts, chain_and_intra)
    each(chunks, intra_chunk, head_start + parts)

    def settle(i):
        h = core * half + i
        early, _ = chip_states(i)
        enters = fade(h, F32(2 * rows), j_skip) * p_recv[i].astype(F32) + x_recv[i].astype(F32)
        second = fade(h, F32(rows), j_first) * enters + early
        carry_ref[i] = jnp.where(is_second, second, enters)
        c_send[i] = jnp.where(is_second, enters, second).astype(BF16)

    def finish(h, enters):
        reach = jnp.exp(reach_ref[...] * (-slopes_ref[h]))
        for b in range(blocks):
            here = pl.ds(b * BLOCK, BLOCK)
            inter = jnp.dot(q_ref[here, cols(h)], enters.astype(BF16), preferred_element_type=F32)
            mixed = mixed_ref[here, cols(h)] + inter * (reach * lead_ref[b])
            sq_ref[here, :] += mixed * mixed
            out_ref[here, cols(h)] = mixed.astype(BF16)
            if b < blocks - 1:
                enters = fade(h, F32(BLOCK), within[b]) * enters + local_ref[b, h]

    def settle_chunk(c):
        x_copy(c, p_recv).wait_recv()
        each((c + 1) * step, settle, c * step)
        c_copy(c).start()
        each((c + 1) * step, lambda i: finish(core * half + i, carry_ref[i]), c * step)
        store(parts + c).start()

    each(parts, settle_chunk)

    def last_chunk(c):
        c_copy(c).wait_recv()
        each((c + 1) * step, lambda i: finish(first + i, c_recv[i].astype(F32)), c * step)
        store(c).start()

    each(parts, last_chunk)

    ones = jnp.ones((8, size), F32)
    summed = lax.dot_general(
        ones, sq_ref[...], (((1,), (1,)), ((), ())),
        precision=lax.Precision.HIGHEST, preferred_element_type=F32,
    )
    sq_send[...] = summed

    def sq_copy(i):
        return pltpu.make_async_remote_copy(
            src_ref=sq_send, dst_ref=sq_recv.at[i], send_sem=sq_out.at[i], recv_sem=sq_in.at[i],
            device_id={"head": lax.rem(headpos + i, head_parts)}, device_id_type=MESH,
        )

    for i in range(1, head_parts):
        sq_copy(i).start()

    def drain(c):
        s_copy(c).wait_send()
        x_copy(c, p_send).wait_send()
        c_copy(c).wait_send()

        @pl.when(plane < planes - 1)
        def _():
            p_copy(c).wait_send()

    each(parts, drain)
    for i in range(1, head_parts):
        sq_copy(i).wait_recv()
        summed = summed + sq_recv[i]
    inverse = lax.rsqrt(summed / F32(heads * size * head_parts) + F32(1e-05))
    inv_ref[...] = jnp.broadcast_to(jnp.transpose(inverse)[:, 0:1], inv_ref.shape)
    for i in range(1, head_parts):
        sq_copy(i).wait_send()
    each(chunks, lambda oc: store(oc).wait())


def shards(planes, head_parts, queries, key_rows, values, slopes, doc_lengths, norm_gain):
    rows, feat = queries.shape
    heads = slopes.shape[0]
    size = feat // heads
    blocks = rows // BLOCK
    half = heads // 2
    parts = min(4, half)
    hbm = pl.BlockSpec(memory_space=pl.ANY)
    smem = pl.BlockSpec(memory_space=pltpu.SMEM)
    states = lambda dtype: pltpu.VMEM((half, size, size), dtype)
    dma = lambda n: pltpu.SemaphoreType.DMA((n,))
    mixed, inverse = pl.pallas_call(
        functools.partial(kernel, planes, head_parts, heads, blocks, parts),
        out_shape=(
            jax.ShapeDtypeStruct((rows, feat), BF16),
            jax.ShapeDtypeStruct((rows, size), F32),
        ),
        in_specs=[smem, smem, hbm, hbm, hbm],
        out_specs=(hbm, pl.BlockSpec(memory_space=pltpu.VMEM)),
        scratch_shapes=[
            pltpu.VMEM((rows, feat), BF16),
            pltpu.VMEM((rows, feat), BF16),
            pltpu.VMEM((rows, feat), BF16),
            pltpu.VMEM((rows, feat), F32),
            pltpu.VMEM((rows, feat), BF16),
            pltpu.VMEM((max(blocks - 1, 1), heads, size, size), F32),
            states(F32),
            states(F32),
            *[states(BF16)] * 7,
            pltpu.VMEM((BLOCK, BLOCK), F32),
            pltpu.VMEM((blocks, BLOCK, BLOCK), F32),
            pltpu.VMEM((blocks, BLOCK, size), F32),
            pltpu.VMEM((blocks, BLOCK, size), F32),
            pltpu.VMEM((BLOCK, size), F32),
            pltpu.VMEM((BLOCK, size), F32),
            pltpu.VMEM((rows, size), F32),
            pltpu.VMEM((8, rows), F32),
            pltpu.VMEM((head_parts, 8, rows), F32),
            *[dma(2 * parts)] * 4,
            *[dma(parts)] * 8,
            dma(head_parts),
            dma(head_parts),
        ],
        compiler_params=pltpu.CompilerParams(
            collective_id=0, has_side_effects=True, vmem_limit_bytes=56 * 1024 * 1024
        ),
    )(slopes, doc_lengths, queries, key_rows, values)
    return (mixed.astype(F32) * inverse[:, :1] * norm_gain[None, :]).astype(BF16)


def solution(mesh):
    placed = (P("seq", "head"), P("seq", "head"), P("seq", "head"), P("head"), P(), P("head"))
    return jax.shard_map(
        functools.partial(shards, mesh.shape["seq"] // 4, mesh.shape["head"]),
        mesh=mesh, in_specs=placed, out_specs=P("seq", "head"), check_vma=False,
    )
```

```python
import functools

import jax
import jax.numpy as jnp
from jax import lax
from jax.experimental import pallas as pl
from jax.experimental.pallas import tpu as pltpu
from jax.sharding import PartitionSpec as P

BLOCK = 256
FAR = 1e30
LOG2E = 1.4426950408889634
F32 = jnp.float32
BF16 = jnp.bfloat16
MESH = pl.DeviceIdType.MESH


def kernel(
    planes, head_parts, heads, blocks, parts,
    slopes_ref, docs_ref, q_hbm, k_hbm, v_hbm,
    mixed_hbm, inv_ref,
    q_ref, k_ref, v_ref, mixed_ref, out_ref, local_ref, own_ref, carry_ref,
    s_send, s_recv, p_send, p_recv, x_recv, c_send, c_recv,
    lag_ref, same_ref, tail_ref, lead_ref, rem_ref, reach_ref, sq_ref, sq_send, sq_recv,
    q_sem, k_sem, v_sem, o_sem,
    s_out, s_in, p_out, p_in, x_out, x_in, c_out, c_in, sq_out, sq_in,
):
    half = heads // 2
    step = half // parts
    chunks = 2 * parts
    rows = blocks * BLOCK
    size = q_ref.shape[1] // heads
    seq = lax.axis_index("seq")
    headpos = lax.axis_index("head")
    core = lax.rem(seq, 2)
    side = lax.rem(lax.div(seq, 2), 2)
    plane = lax.div(seq, 4)
    partner = seq + 1 - 2 * core
    across = seq + 2 - 4 * side
    ahead = jnp.minimum(seq + 4, 4 * planes - 1)
    first = (1 - core) * half

    def head_of(o):
        return lax.rem(o + first, heads)

    def cols(h):
        return pl.ds(pl.multiple_of(h * size, size), size)

    def wide(oc):
        return pl.ds(pl.multiple_of(head_of(oc * step) * size, step * size), step * size)

    def load(hbm, ref, sem, oc):
        return pltpu.make_async_copy(hbm.at[:, wide(oc)], ref.at[:, wide(oc)], sem.at[oc])

    def store(oc):
        return pltpu.make_async_copy(out_ref.at[:, wide(oc)], mixed_hbm.at[:, wide(oc)], o_sem.at[oc])

    def piece(c):
        return pl.ds(c * step, step)

    def remote(src, dst, c, out_sem, in_sem, target):
        return pltpu.make_async_remote_copy(
            src_ref=src.at[piece(c)], dst_ref=dst.at[piece(c)],
            send_sem=out_sem.at[c], recv_sem=in_sem.at[c],
            device_id={"seq": target}, device_id_type=MESH,
        )

    def s_copy(c):
        return remote(s_send, s_recv, c, s_out, s_in, partner)

    def p_copy(c):
        return remote(p_send, p_recv, c, p_out, p_in, ahead)

    def x_copy(c, src):
        return remote(src, x_recv, c, x_out, x_in, across)

    def c_copy(c):
        return remote(c_send, c_recv, c, c_out, c_in, partner)

    def each(count, body, start=0):
        def turn(i, _):
            body(i)
            return 0
        lax.fori_loop(start, count, turn, 0)

    def grouped(c, body):
        for i in range(step):
            body(c * step + i)

    barrier = pltpu.get_barrier_semaphore()
    pl.semaphore_signal(barrier, inc=1, device_id={"seq": partner}, device_id_type=MESH)
    pl.semaphore_signal(barrier, inc=1, device_id={"seq": across}, device_id_type=MESH)

    @pl.when(plane < planes - 1)
    def _():
        pl.semaphore_signal(barrier, inc=1, device_id={"seq": seq + 4}, device_id_type=MESH)

    @pl.when(plane > 0)
    def _():
        pl.semaphore_signal(barrier, inc=1, device_id={"seq": seq - 4}, device_id_type=MESH)

    for i in range(1, head_parts):
        pl.semaphore_signal(
            barrier, inc=1, device_id={"head": lax.rem(headpos + i, head_parts)}, device_id_type=MESH
        )

    def begin_kv(oc):
        load(k_hbm, k_ref, k_sem, oc).start()
        load(v_hbm, v_ref, v_sem, oc).start()

    each(chunks, begin_kv)
    each(chunks, lambda oc: load(q_hbm, q_ref, q_sem, oc).start())

    starts = []
    total = jnp.int32(0)
    for j in range(docs_ref.shape[0] - 1):
        total = total + docs_ref[j]
        starts.append(total)

    def segment(pos):
        counted = jnp.zeros_like(pos)
        for s in starts:
            counted = counted + jnp.where(pos >= s, 1, 0)
        return jnp.where(pos < 0, -1, counted)

    def joined(a, b):
        return jnp.where(segment(a) == segment(b), F32(1), F32(0))

    base = seq * rows
    chip = base - core * rows
    down = lax.broadcasted_iota(jnp.int32, (BLOCK, BLOCK), 0)
    along = lax.broadcasted_iota(jnp.int32, (BLOCK, BLOCK), 1)
    lag = jnp.where(down >= along, (down - along).astype(F32), F32(FAR))
    lag_ref[...] = lag[BLOCK // 2:]
    offs = lax.broadcasted_iota(jnp.int32, (BLOCK, size), 0)
    rem_ref[...] = (BLOCK - 1 - offs).astype(F32)
    reach_ref[...] = (offs + 1).astype(F32)
    within = []
    for b in range(blocks):
        b0 = base + b * BLOCK
        row_seg = segment(b0 + offs)
        same_ref[b] = jnp.where(segment(b0 + down) == segment(b0 + along), F32(1), F32(0))
        tail_ref[b] = jnp.where(row_seg == segment(b0 + BLOCK - 1), F32(1), F32(0))
        lead_ref[b] = jnp.where(row_seg == segment(b0 - 1), F32(1), F32(0))
        within.append(joined(b0 - 1, b0 + BLOCK - 1))
    j_cores = joined(chip + rows - 1, chip + 2 * rows - 1)
    j_first = joined(chip - 1, chip + rows - 1)
    j_chain = joined(chip - 2 * rows - 1, chip + 2 * rows - 1)
    j_skip = joined(chip - 2 * rows - 1, chip - 1)

    def rate(h):
        return slopes_ref[h] * F32(-LOG2E)

    def fade(h, distance, keep):
        return jnp.exp2(jnp.full((1, size), rate(h) * distance, F32)) * keep

    sq_ref[...] = jnp.zeros_like(sq_ref)

    @pl.when(plane == 0)
    def _():
        p_recv[...] = jnp.zeros_like(p_recv)

    def end_state(h):
        scale = jnp.exp2(rem_ref[...] * rate(h))
        state = None
        for b in range(blocks):
            here = pl.ds(b * BLOCK, BLOCK)
            weighted = (scale * tail_ref[b] * v_ref[here, cols(h)].astype(F32)).astype(BF16)
            one = lax.dot_general(
                k_ref[here, cols(h)], weighted, (((0,), (0,)), ((), ())), preferred_element_type=F32
            )
            if b < blocks - 1:
                local_ref[b, h] = one
            state = one if state is None else fade(h, F32(BLOCK), within[b]) * state + one
        return state

    def wait_kv(oc):
        load(k_hbm, k_ref, k_sem, oc).wait()
        load(v_hbm, v_ref, v_sem, oc).wait()

    def give(i):
        s_send[i] = end_state(first + i).astype(BF16)

    def keep(i):
        own_ref[i] = end_state(core * half + i)

    def first_chunk(c):
        wait_kv(c)
        grouped(c, give)

    first_chunk(jnp.int32(0))
    beside = jnp.where(plane > 0, 1, 0) + jnp.where(plane < planes - 1, 1, 0)
    pl.semaphore_wait(barrier, 1 + head_parts + beside)
    s_copy(0).start()

    def next_chunk(c):
        first_chunk(c)
        s_copy(c).start()

    each(parts, next_chunk, 1)

    def own_chunk(c):
        wait_kv(parts + c)
        grouped(c, keep)

    each(parts, own_chunk)

    mid = BLOCK // 2

    def intra(h):
        decay = jnp.exp2(lag_ref[...] * rate(h))
        for b in range(blocks):
            here = pl.ds(b * BLOCK, BLOCK)
            scores = lax.dot_general(
                q_ref[here, cols(h)], k_ref[here, cols(h)], (((1,), (1,)), ((), ())),
                preferred_element_type=F32,
            )
            upper = (scores[:mid, :mid] * decay[:, mid:] * same_ref[b, :mid, :mid]).astype(BF16)
            lower = (scores[mid:] * decay * same_ref[b, mid:, :]).astype(BF16)
            weights = jnp.concatenate(
                [jnp.concatenate([upper, jnp.zeros((mid, mid), BF16)], axis=1), lower], axis=0
            )
            mixed_ref[here, cols(h)] = jnp.dot(
                weights, v_ref[here, cols(h)], preferred_element_type=F32
            )

    def intra_chunk(oc):
        load(q_hbm, q_ref, q_sem, oc).wait()
        grouped(oc, lambda o: intra(head_of(o)))

    is_second = core == 1

    def chip_states(i):
        mine, other = own_ref[i], s_recv[i].astype(F32)
        return jnp.where(is_second, other, mine), jnp.where(is_second, mine, other)

    def chain(i):
        h = core * half + i
        early, late = chip_states(i)
        chip_state = fade(h, F32(rows), j_cores) * early + late
        p_send[i] = (fade(h, F32(4 * rows), j_chain) * p_recv[i].astype(F32) + chip_state).astype(BF16)

    def chain_chunk(c):
        s_copy(c).wait_recv()

        @pl.when(plane > 0)
        def _():
            p_copy(c).wait_recv()

        @pl.when(side == 1)
        def _():
            x_copy(c, p_recv).start()

        grouped(c, chain)

        @pl.when(plane < planes - 1)
        def _():
            p_copy(c).start()

        @pl.when(side == 0)
        def _():
            x_copy(c, p_send).start()

    head_start = jnp.minimum(plane, parts)
    each(head_start, intra_chunk)

    def chain_and_intra(c):
        chain_chunk(c)
        intra_chunk(head_start + c)

    each(parts, chain_and_intra)
    each(chunks, intra_chunk, head_start + parts)

    def settle(i):
        h = core * half + i
        early, _ = chip_states(i)
        enters = fade(h, F32(2 * rows), j_skip) * p_recv[i].astype(F32) + x_recv[i].astype(F32)
        second = fade(h, F32(rows), j_first) * enters + early
        carry_ref[i] = jnp.where(is_second, second, enters)
        c_send[i] = jnp.where(is_second, enters, second).astype(BF16)

    def finish_all(work):
        fades = [jnp.exp2(reach_ref[...] * rate(h)) for h, _ in work]
        states = [enters for _, enters in work]
        for b in range(blocks):
            here = pl.ds(b * BLOCK, BLOCK)
            squares = sq_ref[here, :]
            for i, (h, _) in enumerate(work):
                inter = jnp.dot(
                    q_ref[here, cols(h)], states[i].astype(BF16), preferred_element_type=F32
                )
                mixed = mixed_ref[here, cols(h)] + inter * (fades[i] * lead_ref[b])
                squares = squares + mixed * mixed
                out_ref[here, cols(h)] = mixed.astype(BF16)
                if b < blocks - 1:
                    states[i] = fade(h, F32(BLOCK), within[b]) * states[i] + local_ref[b, h]
            sq_ref[here, :] = squares

    def settle_chunk(c):
        x_copy(c, p_recv).wait_recv()
        grouped(c, settle)
        c_copy(c).start()
        finish_all([(core * half + c * step + i, carry_ref[c * step + i]) for i in range(step)])
        store(parts + c).start()

    each(parts, settle_chunk)

    def last_chunk(c):
        c_copy(c).wait_recv()
        finish_all([(first + c * step + i, c_recv[c * step + i].astype(F32)) for i in range(step)])
        store(c).start()

    each(parts, last_chunk)

    ones = jnp.ones((8, size), F32)
    summed = lax.dot_general(
        ones, sq_ref[...], (((1,), (1,)), ((), ())),
        precision=lax.Precision.HIGHEST, preferred_element_type=F32,
    )
    sq_send[...] = summed

    def sq_copy(i):
        return pltpu.make_async_remote_copy(
            src_ref=sq_send, dst_ref=sq_recv.at[i], send_sem=sq_out.at[i], recv_sem=sq_in.at[i],
            device_id={"head": lax.rem(headpos + i, head_parts)}, device_id_type=MESH,
        )

    for i in range(1, head_parts):
        sq_copy(i).start()

    def drain(c):
        s_copy(c).wait_send()
        x_copy(c, p_send).wait_send()
        c_copy(c).wait_send()

        @pl.when(plane < planes - 1)
        def _():
            p_copy(c).wait_send()

    each(parts, drain)
    for i in range(1, head_parts):
        sq_copy(i).wait_recv()
        summed = summed + sq_recv[i]
    inverse = lax.rsqrt(summed / F32(heads * size * head_parts) + F32(1e-05))
    inv_ref[...] = jnp.broadcast_to(jnp.transpose(inverse)[:, 0:1], inv_ref.shape)
    for i in range(1, head_parts):
        sq_copy(i).wait_send()
    each(chunks, lambda oc: store(oc).wait())


def scale_kernel(mixed_ref, inv_ref, gain_ref, out_ref):
    size = inv_ref.shape[1]
    inverse = inv_ref[...]
    for c in range(0, out_ref.shape[1], size):
        piece = mixed_ref[:, c:c + size].astype(F32)
        out_ref[:, c:c + size] = (piece * inverse * gain_ref[:, c:c + size]).astype(BF16)


def shards(planes, head_parts, queries, key_rows, values, slopes, doc_lengths, norm_gain):
    rows, feat = queries.shape
    heads = slopes.shape[0]
    size = feat // heads
    blocks = rows // BLOCK
    half = heads // 2
    parts = min(4, half)
    hbm = pl.BlockSpec(memory_space=pl.ANY)
    smem = pl.BlockSpec(memory_space=pltpu.SMEM)
    states = lambda dtype: pltpu.VMEM((half, size, size), dtype)
    dma = lambda n: pltpu.SemaphoreType.DMA((n,))
    mixed, inverse = pl.pallas_call(
        functools.partial(kernel, planes, head_parts, heads, blocks, parts),
        out_shape=(
            jax.ShapeDtypeStruct((rows, feat), BF16),
            jax.ShapeDtypeStruct((rows, size), F32),
        ),
        in_specs=[smem, smem, hbm, hbm, hbm],
        out_specs=(hbm, pl.BlockSpec(memory_space=pltpu.VMEM)),
        scratch_shapes=[
            pltpu.VMEM((rows, feat), BF16),
            pltpu.VMEM((rows, feat), BF16),
            pltpu.VMEM((rows, feat), BF16),
            pltpu.VMEM((rows, feat), F32),
            pltpu.VMEM((rows, feat), BF16),
            pltpu.VMEM((max(blocks - 1, 1), heads, size, size), F32),
            states(F32),
            states(F32),
            *[states(BF16)] * 7,
            pltpu.VMEM((BLOCK // 2, BLOCK), F32),
            pltpu.VMEM((blocks, BLOCK, BLOCK), F32),
            pltpu.VMEM((blocks, BLOCK, size), F32),
            pltpu.VMEM((blocks, BLOCK, size), F32),
            pltpu.VMEM((BLOCK, size), F32),
            pltpu.VMEM((BLOCK, size), F32),
            pltpu.VMEM((rows, size), F32),
            pltpu.VMEM((8, rows), F32),
            pltpu.VMEM((head_parts, 8, rows), F32),
            *[dma(2 * parts)] * 4,
            *[dma(parts)] * 8,
            dma(head_parts),
            dma(head_parts),
        ],
        compiler_params=pltpu.CompilerParams(
            collective_id=0, has_side_effects=True, vmem_limit_bytes=56 * 1024 * 1024
        ),
    )(slopes, doc_lengths, queries, key_rows, values)
    width = feat // 8
    return pl.pallas_call(
        scale_kernel,
        out_shape=jax.ShapeDtypeStruct((rows, feat), BF16),
        grid=(feat // width,),
        in_specs=[
            pl.BlockSpec((rows, width), lambda i: (0, i)),
            pl.BlockSpec((rows, size), lambda i: (0, 0)),
            pl.BlockSpec((1, width), lambda i: (0, i)),
        ],
        out_specs=pl.BlockSpec((rows, width), lambda i: (0, i)),
    )(mixed, inverse, norm_gain.reshape(1, feat))


def solution(mesh):
    placed = (P("seq", "head"), P("seq", "head"), P("seq", "head"), P("head"), P(), P("head"))
    return jax.shard_map(
        functools.partial(shards, mesh.shape["seq"] // 4, mesh.shape["head"]),
        mesh=mesh, in_specs=placed, out_specs=P("seq", "head"), check_vma=False,
    )
```

```python
import functools

import jax
import jax.numpy as jnp
from jax import lax
from jax.experimental import pallas as pl
from jax.experimental.pallas import tpu as pltpu
from jax.sharding import PartitionSpec as P

BLOCK = 256
FAR = 1e30
LOG2E = 1.4426950408889634
F32 = jnp.float32
BF16 = jnp.bfloat16
MESH = pl.DeviceIdType.MESH


def kernel(
    planes, head_parts, heads, blocks, step, few,
    slopes_ref, docs_ref, q_hbm, k_hbm, v_hbm,
    mixed_hbm, inv_ref,
    q_ref, k_ref, v_ref, mixed_ref, out_ref, local_ref, own_ref, carry_ref, chip_ref,
    s_send, s_recv, c_send, c_recv, a_send, a_recv, p_send, p_recv, x_send, x_recv,
    lag_ref, same_ref, tail_ref, lead_ref, rem_ref, reach_ref, sq_ref, sq_send, sq_recv,
    q_sem, k_sem, v_sem, o_sem,
    s_out, s_in, c_out, c_in, a_out, a_in, p_out, p_in, x_out, x_in, sq_out, sq_in,
):
    half = heads // 2
    quarter = half // 2
    parts = half // step
    chunks = 2 * parts
    turns = quarter // few
    rows = blocks * BLOCK
    size = q_ref.shape[1] // heads
    seq = lax.axis_index("seq")
    headpos = lax.axis_index("head")
    core = lax.rem(seq, 2)
    side = lax.rem(lax.div(seq, 2), 2)
    plane = lax.div(seq, 4)
    partner = seq + 1 - 2 * core
    across = seq + 2 - 4 * side
    ahead = jnp.minimum(seq + 4, 4 * planes - 1)
    far = (1 - side) * quarter

    def mine(u):
        return core * half + lax.rem(u + far, half)

    def theirs(u):
        return (1 - core) * half + lax.rem(u + far, half)

    def head_of(o):
        group = jnp.where(o >= half, core, 1 - core)
        return group * half + lax.rem(lax.rem(o, half) + far, half)

    def cols(h):
        return pl.ds(pl.multiple_of(h * size, size), size)

    def wide(oc):
        return pl.ds(pl.multiple_of(head_of(oc * step) * size, step * size), step * size)

    def load(hbm, ref, sem, oc):
        return pltpu.make_async_copy(hbm.at[:, wide(oc)], ref.at[:, wide(oc)], sem.at[oc])

    def store(oc):
        return pltpu.make_async_copy(out_ref.at[:, wide(oc)], mixed_hbm.at[:, wide(oc)], o_sem.at[oc])

    def remote(src, dst, c, count, out_sem, in_sem, target):
        piece = pl.ds(c * count, count)
        return pltpu.make_async_remote_copy(
            src_ref=src.at[piece], dst_ref=dst.at[piece],
            send_sem=out_sem.at[c], recv_sem=in_sem.at[c],
            device_id={"seq": target}, device_id_type=MESH,
        )

    def s_copy(c):
        return remote(s_send, s_recv, c, step, s_out, s_in, partner)

    def c_copy(c):
        return remote(c_send, c_recv, c, few, c_out, c_in, partner)

    def a_copy(c):
        return remote(a_send, a_recv, c, few, a_out, a_in, across)

    def p_copy(c):
        return remote(p_send, p_recv, c, few, p_out, p_in, ahead)

    def x_copy(c):
        return remote(x_send, x_recv, c, few, x_out, x_in, across)

    def each(count, body, start=0):
        def turn(i, _):
            body(i)
            return 0
        lax.fori_loop(start, count, turn, 0)

    def grouped(c, body, count=step):
        for i in range(count):
            body(c * count + i)

    barrier = pltpu.get_barrier_semaphore()
    pl.semaphore_signal(barrier, inc=1, device_id={"seq": partner}, device_id_type=MESH)
    pl.semaphore_signal(barrier, inc=1, device_id={"seq": across}, device_id_type=MESH)

    @pl.when(plane < planes - 1)
    def _():
        pl.semaphore_signal(barrier, inc=1, device_id={"seq": seq + 4}, device_id_type=MESH)

    @pl.when(plane > 0)
    def _():
        pl.semaphore_signal(barrier, inc=1, device_id={"seq": seq - 4}, device_id_type=MESH)

    for i in range(1, head_parts):
        pl.semaphore_signal(
            barrier, inc=1, device_id={"head": lax.rem(headpos + i, head_parts)}, device_id_type=MESH
        )

    def begin_kv(oc):
        load(k_hbm, k_ref, k_sem, oc).start()
        load(v_hbm, v_ref, v_sem, oc).start()

    each(chunks, begin_kv)
    each(chunks, lambda oc: load(q_hbm, q_ref, q_sem, oc).start())

    starts = []
    total = jnp.int32(0)
    for j in range(docs_ref.shape[0] - 1):
        total = total + docs_ref[j]
        starts.append(total)

    def segment(pos):
        counted = jnp.zeros_like(pos)
        for s in starts:
            counted = counted + jnp.where(pos >= s, 1, 0)
        return jnp.where(pos < 0, -1, counted)

    def joined(a, b):
        return jnp.where(segment(a) == segment(b), F32(1), F32(0))

    base = seq * rows
    chip = base - core * rows
    down = lax.broadcasted_iota(jnp.int32, (BLOCK, BLOCK), 0)
    along = lax.broadcasted_iota(jnp.int32, (BLOCK, BLOCK), 1)
    lag = jnp.where(down >= along, (down - along).astype(F32), F32(FAR))
    lag_ref[...] = lag[BLOCK // 2:]
    offs = lax.broadcasted_iota(jnp.int32, (BLOCK, size), 0)
    rem_ref[...] = (BLOCK - 1 - offs).astype(F32)
    reach_ref[...] = (offs + 1).astype(F32)
    within = []
    for b in range(blocks):
        b0 = base + b * BLOCK
        row_seg = segment(b0 + offs)
        same_ref[b] = jnp.where(segment(b0 + down) == segment(b0 + along), F32(1), F32(0))
        tail_ref[b] = jnp.where(row_seg == segment(b0 + BLOCK - 1), F32(1), F32(0))
        lead_ref[b] = jnp.where(row_seg == segment(b0 - 1), F32(1), F32(0))
        within.append(joined(b0 - 1, b0 + BLOCK - 1))
    board = chip - 2 * side * rows
    j_cores = joined(chip + rows - 1, chip + 2 * rows - 1)
    j_enter = joined(chip - 1, chip + rows - 1)
    j_chips = joined(board + 2 * rows - 1, board + 4 * rows - 1)
    j_board = joined(board - 1, board + 4 * rows - 1)
    j_front = joined(board - 1, board + 2 * rows - 1)

    def rate(h):
        return slopes_ref[h] * F32(-LOG2E)

    def fade(h, distance, keep):
        return jnp.exp2(jnp.full((1, size), rate(h) * distance, F32)) * keep

    sq_ref[...] = jnp.zeros_like(sq_ref)

    @pl.when(plane == 0)
    def _():
        p_recv[...] = jnp.zeros_like(p_recv)

    def end_state(h):
        scale = jnp.exp2(rem_ref[...] * rate(h))
        state = None
        for b in range(blocks):
            here = pl.ds(b * BLOCK, BLOCK)
            weighted = (scale * tail_ref[b] * v_ref[here, cols(h)].astype(F32)).astype(BF16)
            one = lax.dot_general(
                k_ref[here, cols(h)], weighted, (((0,), (0,)), ((), ())), preferred_element_type=F32
            )
            if b < blocks - 1:
                local_ref[b, h] = one
            state = one if state is None else fade(h, F32(BLOCK), within[b]) * state + one
        return state

    def wait_kv(oc):
        load(k_hbm, k_ref, k_sem, oc).wait()
        load(v_hbm, v_ref, v_sem, oc).wait()

    def give(i):
        s_send[i] = end_state(theirs(i)).astype(BF16)

    def keep(i):
        own_ref[i] = end_state(mine(i))

    def first_chunk(c):
        wait_kv(c)
        grouped(c, give)

    first_chunk(jnp.int32(0))
    beside = jnp.where(plane > 0, 1, 0) + jnp.where(plane < planes - 1, 1, 0)
    pl.semaphore_wait(barrier, 1 + head_parts + beside)
    s_copy(0).start()

    def next_chunk(c):
        first_chunk(c)
        s_copy(c).start()

    each(parts, next_chunk, 1)

    def own_chunk(c):
        wait_kv(parts + c)
        grouped(c, keep)

    each(parts, own_chunk)

    mid = BLOCK // 2

    def intra(h):
        decay = jnp.exp2(lag_ref[...] * rate(h))
        for b in range(blocks):
            here = pl.ds(b * BLOCK, BLOCK)
            scores = lax.dot_general(
                q_ref[here, cols(h)], k_ref[here, cols(h)], (((1,), (1,)), ((), ())),
                preferred_element_type=F32,
            )
            upper = (scores[:mid, :mid] * decay[:, mid:] * same_ref[b, :mid, :mid]).astype(BF16)
            lower = (scores[mid:] * decay * same_ref[b, mid:, :]).astype(BF16)
            weights = jnp.concatenate(
                [jnp.concatenate([upper, jnp.zeros((mid, mid), BF16)], axis=1), lower], axis=0
            )
            mixed_ref[here, cols(h)] = jnp.dot(
                weights, v_ref[here, cols(h)], preferred_element_type=F32
            )

    def intra_chunk(oc):
        load(q_hbm, q_ref, q_sem, oc).wait()
        grouped(oc, lambda o: intra(head_of(o)))

    is_second = core == 1
    is_after = side == 1

    def core_states(u):
        here, there = own_ref[u], s_recv[u].astype(F32)
        return jnp.where(is_second, there, here), jnp.where(is_second, here, there)

    def chip_state(u):
        early, late = core_states(u)
        return fade(mine(u), F32(rows), j_cores) * early + late

    def give_chip(w):
        a_send[w] = chip_state(w).astype(BF16)

    def keep_chip(w):
        chip_ref[w] = chip_state(quarter + w)

    def give_chunk(c):
        s_copy(c).wait_recv()
        grouped(c, give_chip)
        for i in range(step // few):
            a_copy(c * (step // few) + i).start()

    each(parts // 2, give_chunk)

    def keep_chunk(c):
        s_copy(parts // 2 + c).wait_recv()
        grouped(c, keep_chip)

    each(parts // 2, keep_chunk)

    def settle(u, enters):
        early, _ = core_states(u)
        second = fade(mine(u), F32(rows), j_enter) * enters + early
        carry_ref[u] = jnp.where(is_second, second, enters)
        c_send[u] = jnp.where(is_second, enters, second).astype(BF16)

    def chain(w):
        h = mine(quarter + w)
        here, there = chip_ref[w], a_recv[w].astype(F32)
        early, late = jnp.where(is_after, there, here), jnp.where(is_after, here, there)
        before = p_recv[w].astype(F32)
        total = fade(h, F32(2 * rows), j_chips) * early + late
        p_send[w] = (fade(h, F32(4 * rows), j_board) * before + total).astype(BF16)
        second = fade(h, F32(2 * rows), j_front) * before + early
        x_send[w] = jnp.where(is_after, before, second).astype(BF16)
        settle(quarter + w, jnp.where(is_after, second, before))

    def chain_chunk(c):
        a_copy(c).wait_recv()

        @pl.when(plane > 0)
        def _():
            p_copy(c).wait_recv()

        grouped(c, chain, few)

        @pl.when(plane < planes - 1)
        def _():
            p_copy(c).start()

        x_copy(c).start()
        c_copy(turns + c).start()

    def across_chunk(c):
        x_copy(c).wait_recv()
        grouped(c, lambda w: settle(w, x_recv[w].astype(F32)), few)
        c_copy(c).start()

    ready = jnp.minimum(2 + 2 * plane, chunks)
    each(ready, intra_chunk)
    each(turns, chain_chunk)
    each(chunks, intra_chunk, ready)
    each(turns, across_chunk)

    def finish_all(work):
        fades = [jnp.exp2(reach_ref[...] * rate(h)) for h, _ in work]
        states = [enters for _, enters in work]
        for b in range(blocks):
            here = pl.ds(b * BLOCK, BLOCK)
            squares = sq_ref[here, :]
            for i, (h, _) in enumerate(work):
                inter = jnp.dot(
                    q_ref[here, cols(h)], states[i].astype(BF16), preferred_element_type=F32
                )
                mixed = mixed_ref[here, cols(h)] + inter * (fades[i] * lead_ref[b])
                squares = squares + mixed * mixed
                out_ref[here, cols(h)] = mixed.astype(BF16)
                if b < blocks - 1:
                    states[i] = fade(h, F32(BLOCK), within[b]) * states[i] + local_ref[b, h]
            sq_ref[here, :] = squares

    def own_part(c):
        finish_all([(mine(c * step + i), carry_ref[c * step + i]) for i in range(step)])
        store(parts + c).start()

    each(parts, own_part)

    def other_part(c):
        for i in range(step // few):
            c_copy(c * (step // few) + i).wait_recv()
        finish_all(
            [(theirs(c * step + i), c_recv[c * step + i].astype(F32)) for i in range(step)]
        )
        store(c).start()

    each(parts, other_part)

    ones = jnp.ones((8, size), F32)
    summed = lax.dot_general(
        ones, sq_ref[...], (((1,), (1,)), ((), ())),
        precision=lax.Precision.HIGHEST, preferred_element_type=F32,
    )
    sq_send[...] = summed

    def sq_copy(i):
        return pltpu.make_async_remote_copy(
            src_ref=sq_send, dst_ref=sq_recv.at[i], send_sem=sq_out.at[i], recv_sem=sq_in.at[i],
            device_id={"head": lax.rem(headpos + i, head_parts)}, device_id_type=MESH,
        )

    for i in range(1, head_parts):
        sq_copy(i).start()

    each(parts, lambda c: s_copy(c).wait_send())
    each(2 * turns, lambda c: c_copy(c).wait_send())

    def drain(c):
        a_copy(c).wait_send()
        x_copy(c).wait_send()

        @pl.when(plane < planes - 1)
        def _():
            p_copy(c).wait_send()

    each(turns, drain)
    for i in range(1, head_parts):
        sq_copy(i).wait_recv()
        summed = summed + sq_recv[i]
    inverse = lax.rsqrt(summed / F32(heads * size * head_parts) + F32(1e-05))
    inv_ref[...] = jnp.broadcast_to(jnp.transpose(inverse)[:, 0:1], inv_ref.shape)
    for i in range(1, head_parts):
        sq_copy(i).wait_send()
    each(chunks, lambda oc: store(oc).wait())


def scale_kernel(mixed_ref, inv_ref, gain_ref, out_ref):
    size = inv_ref.shape[1]
    inverse = inv_ref[...]
    for c in range(0, out_ref.shape[1], size):
        piece = mixed_ref[:, c:c + size].astype(F32)
        out_ref[:, c:c + size] = (piece * inverse * gain_ref[:, c:c + size]).astype(BF16)


def shards(planes, head_parts, queries, key_rows, values, slopes, doc_lengths, norm_gain):
    rows, feat = queries.shape
    heads = slopes.shape[0]
    size = feat // heads
    blocks = rows // BLOCK
    half = heads // 2
    quarter = half // 2
    step = min(4, quarter)
    few = max(1, quarter // 4)
    parts = half // step
    turns = quarter // few
    hbm = pl.BlockSpec(memory_space=pl.ANY)
    smem = pl.BlockSpec(memory_space=pltpu.SMEM)
    states = lambda count, dtype: pltpu.VMEM((count, size, size), dtype)
    dma = lambda n: pltpu.SemaphoreType.DMA((n,))
    mixed, inverse = pl.pallas_call(
        functools.partial(kernel, planes, head_parts, heads, blocks, step, few),
        out_shape=(
            jax.ShapeDtypeStruct((rows, feat), BF16),
            jax.ShapeDtypeStruct((rows, size), F32),
        ),
        in_specs=[smem, smem, hbm, hbm, hbm],
        out_specs=(hbm, pl.BlockSpec(memory_space=pltpu.VMEM)),
        scratch_shapes=[
            pltpu.VMEM((rows, feat), BF16),
            pltpu.VMEM((rows, feat), BF16),
            pltpu.VMEM((rows, feat), BF16),
            pltpu.VMEM((rows, feat), F32),
            pltpu.VMEM((rows, feat), BF16),
            pltpu.VMEM((max(blocks - 1, 1), heads, size, size), F32),
            states(half, F32),
            states(half, F32),
            states(quarter, F32),
            *[states(half, BF16)] * 4,
            *[states(quarter, BF16)] * 6,
            pltpu.VMEM((BLOCK // 2, BLOCK), F32),
            pltpu.VMEM((blocks, BLOCK, BLOCK), F32),
            pltpu.VMEM((blocks, BLOCK, size), F32),
            pltpu.VMEM((blocks, BLOCK, size), F32),
            pltpu.VMEM((BLOCK, size), F32),
            pltpu.VMEM((BLOCK, size), F32),
            pltpu.VMEM((rows, size), F32),
            pltpu.VMEM((8, rows), F32),
            pltpu.VMEM((head_parts, 8, rows), F32),
            *[dma(2 * parts)] * 4,
            *[dma(parts)] * 2,
            *[dma(2 * turns)] * 2,
            *[dma(turns)] * 6,
            dma(head_parts),
            dma(head_parts),
        ],
        compiler_params=pltpu.CompilerParams(
            collective_id=0, has_side_effects=True, vmem_limit_bytes=56 * 1024 * 1024
        ),
    )(slopes, doc_lengths, queries, key_rows, values)
    width = feat // 8
    return pl.pallas_call(
        scale_kernel,
        out_shape=jax.ShapeDtypeStruct((rows, feat), BF16),
        grid=(feat // width,),
        in_specs=[
            pl.BlockSpec((rows, width), lambda i: (0, i)),
            pl.BlockSpec((rows, size), lambda i: (0, 0)),
            pl.BlockSpec((1, width), lambda i: (0, i)),
        ],
        out_specs=pl.BlockSpec((rows, width), lambda i: (0, i)),
    )(mixed, inverse, norm_gain.reshape(1, feat))


def solution(mesh):
    placed = (P("seq", "head"), P("seq", "head"), P("seq", "head"), P("head"), P(), P("head"))
    return jax.shard_map(
        functools.partial(shards, mesh.shape["seq"] // 4, mesh.shape["head"]),
        mesh=mesh, in_specs=placed, out_specs=P("seq", "head"), check_vma=False,
    )
```

```python
import functools

import jax
import jax.numpy as jnp
from jax import lax
from jax.experimental import pallas as pl
from jax.experimental.pallas import tpu as pltpu
from jax.sharding import PartitionSpec as P

BLOCK = 256
FAR = 1e30
LOG2E = 1.4426950408889634
F32 = jnp.float32
BF16 = jnp.bfloat16
MESH = pl.DeviceIdType.MESH


def kernel(
    planes, head_parts, heads, blocks, step, few,
    slopes_ref, docs_ref, q_hbm, k_hbm, v_hbm,
    out_ref, inv_ref,
    q_ref, k_ref, v_ref, mixed_ref, local_ref, own_ref, carry_ref, chip_ref,
    s_send, s_recv, c_send, c_recv, a_send, a_recv, p_send, p_recv, x_send, x_recv,
    lag_ref, same_ref, tail_ref, lead_ref, rem_ref, reach_ref, sq_ref, sq_send, sq_recv,
    q_sem, k_sem, v_sem,
    s_out, s_in, c_out, c_in, a_out, a_in, p_out, p_in, x_out, x_in, sq_out, sq_in,
):
    half = heads // 2
    quarter = half // 2
    parts = half // step
    chunks = 2 * parts
    turns = quarter // few
    rows = blocks * BLOCK
    size = q_ref.shape[1] // heads
    seq = lax.axis_index("seq")
    headpos = lax.axis_index("head")
    core = lax.rem(seq, 2)
    side = lax.rem(lax.div(seq, 2), 2)
    plane = lax.div(seq, 4)
    partner = seq + 1 - 2 * core
    across = seq + 2 - 4 * side
    ahead = jnp.minimum(seq + 4, 4 * planes - 1)
    far = (1 - side) * quarter

    def mine(u):
        return core * half + lax.rem(u + far, half)

    def theirs(u):
        return (1 - core) * half + lax.rem(u + far, half)

    def head_of(o):
        group = jnp.where(o >= half, core, 1 - core)
        return group * half + lax.rem(lax.rem(o, half) + far, half)

    def cols(h):
        return pl.ds(pl.multiple_of(h * size, size), size)

    def wide(oc):
        return pl.ds(pl.multiple_of(head_of(oc * step) * size, step * size), step * size)

    def load(hbm, ref, sem, oc):
        return pltpu.make_async_copy(hbm.at[:, wide(oc)], ref.at[:, wide(oc)], sem.at[oc])

    def remote(src, dst, c, count, out_sem, in_sem, target):
        piece = pl.ds(c * count, count)
        return pltpu.make_async_remote_copy(
            src_ref=src.at[piece], dst_ref=dst.at[piece],
            send_sem=out_sem.at[c], recv_sem=in_sem.at[c],
            device_id={"seq": target}, device_id_type=MESH,
        )

    def s_copy(c):
        return remote(s_send, s_recv, c, step, s_out, s_in, partner)

    def c_copy(c):
        return remote(c_send, c_recv, c, few, c_out, c_in, partner)

    def a_copy(c):
        return remote(a_send, a_recv, c, few, a_out, a_in, across)

    def p_copy(c):
        return remote(p_send, p_recv, c, few, p_out, p_in, ahead)

    def x_copy(c):
        return remote(x_send, x_recv, c, few, x_out, x_in, across)

    def each(count, body, start=0):
        def turn(i, _):
            body(i)
            return 0
        lax.fori_loop(start, count, turn, 0)

    def grouped(c, body, count=step):
        for i in range(count):
            body(c * count + i)

    barrier = pltpu.get_barrier_semaphore()
    pl.semaphore_signal(barrier, inc=1, device_id={"seq": partner}, device_id_type=MESH)
    pl.semaphore_signal(barrier, inc=1, device_id={"seq": across}, device_id_type=MESH)

    @pl.when(plane < planes - 1)
    def _():
        pl.semaphore_signal(barrier, inc=1, device_id={"seq": seq + 4}, device_id_type=MESH)

    @pl.when(plane > 0)
    def _():
        pl.semaphore_signal(barrier, inc=1, device_id={"seq": seq - 4}, device_id_type=MESH)

    for i in range(1, head_parts):
        pl.semaphore_signal(
            barrier, inc=1, device_id={"head": lax.rem(headpos + i, head_parts)}, device_id_type=MESH
        )

    def begin_kv(oc):
        load(k_hbm, k_ref, k_sem, oc).start()
        load(v_hbm, v_ref, v_sem, oc).start()

    each(chunks, begin_kv)
    each(chunks, lambda oc: load(q_hbm, q_ref, q_sem, oc).start())

    starts = []
    total = jnp.int32(0)
    for j in range(docs_ref.shape[0] - 1):
        total = total + docs_ref[j]
        starts.append(total)

    def segment(pos):
        counted = jnp.zeros_like(pos)
        for s in starts:
            counted = counted + jnp.where(pos >= s, 1, 0)
        return jnp.where(pos < 0, -1, counted)

    def joined(a, b):
        return jnp.where(segment(a) == segment(b), F32(1), F32(0))

    base = seq * rows
    chip = base - core * rows
    down = lax.broadcasted_iota(jnp.int32, (BLOCK, BLOCK), 0)
    along = lax.broadcasted_iota(jnp.int32, (BLOCK, BLOCK), 1)
    lag = jnp.where(down >= along, (down - along).astype(F32), F32(FAR))
    lag_ref[...] = lag[BLOCK // 2:]
    offs = lax.broadcasted_iota(jnp.int32, (BLOCK, size), 0)
    rem_ref[...] = (BLOCK - 1 - offs).astype(F32)
    reach_ref[...] = (offs + 1).astype(F32)
    within = []
    for b in range(blocks):
        b0 = base + b * BLOCK
        row_seg = segment(b0 + offs)
        same_ref[b] = jnp.where(segment(b0 + down) == segment(b0 + along), F32(1), F32(0))
        tail_ref[b] = jnp.where(row_seg == segment(b0 + BLOCK - 1), F32(1), F32(0))
        lead_ref[b] = jnp.where(row_seg == segment(b0 - 1), F32(1), F32(0))
        within.append(joined(b0 - 1, b0 + BLOCK - 1))
    board = chip - 2 * side * rows
    j_cores = joined(chip + rows - 1, chip + 2 * rows - 1)
    j_enter = joined(chip - 1, chip + rows - 1)
    j_chips = joined(board + 2 * rows - 1, board + 4 * rows - 1)
    j_board = joined(board - 1, board + 4 * rows - 1)
    j_front = joined(board - 1, board + 2 * rows - 1)

    def rate(h):
        return slopes_ref[h] * F32(-LOG2E)

    def fade(h, distance, keep):
        return jnp.exp2(jnp.full((1, size), rate(h) * distance, F32)) * keep

    sq_ref[...] = jnp.zeros_like(sq_ref)

    @pl.when(plane == 0)
    def _():
        p_recv[...] = jnp.zeros_like(p_recv)

    def end_state(h):
        scale = jnp.exp2(rem_ref[...] * rate(h))
        state = None
        for b in range(blocks):
            here = pl.ds(b * BLOCK, BLOCK)
            weighted = (scale * tail_ref[b] * v_ref[here, cols(h)].astype(F32)).astype(BF16)
            one = lax.dot_general(
                k_ref[here, cols(h)], weighted, (((0,), (0,)), ((), ())), preferred_element_type=F32
            )
            if b < blocks - 1:
                local_ref[b, h] = one
            state = one if state is None else fade(h, F32(BLOCK), within[b]) * state + one
        return state

    def wait_kv(oc):
        load(k_hbm, k_ref, k_sem, oc).wait()
        load(v_hbm, v_ref, v_sem, oc).wait()

    def give(i):
        s_send[i] = end_state(theirs(i)).astype(BF16)

    def keep(i):
        own_ref[i] = end_state(mine(i))

    def first_chunk(c):
        wait_kv(c)
        grouped(c, give)

    first_chunk(jnp.int32(0))
    beside = jnp.where(plane > 0, 1, 0) + jnp.where(plane < planes - 1, 1, 0)
    pl.semaphore_wait(barrier, 1 + head_parts + beside)
    s_copy(0).start()

    def next_chunk(c):
        first_chunk(c)
        s_copy(c).start()

    each(parts, next_chunk, 1)

    def own_chunk(c):
        wait_kv(parts + c)
        grouped(c, keep)

    each(parts, own_chunk)

    mid = BLOCK // 2

    def intra(h):
        decay = jnp.exp2(lag_ref[...] * rate(h))
        for b in range(blocks):
            here = pl.ds(b * BLOCK, BLOCK)
            scores = lax.dot_general(
                q_ref[here, cols(h)], k_ref[here, cols(h)], (((1,), (1,)), ((), ())),
                preferred_element_type=F32,
            )
            upper = (scores[:mid, :mid] * decay[:, mid:] * same_ref[b, :mid, :mid]).astype(BF16)
            lower = (scores[mid:] * decay * same_ref[b, mid:, :]).astype(BF16)
            weights = jnp.concatenate(
                [jnp.concatenate([upper, jnp.zeros((mid, mid), BF16)], axis=1), lower], axis=0
            )
            mixed_ref[here, cols(h)] = jnp.dot(
                weights, v_ref[here, cols(h)], preferred_element_type=F32
            )

    def intra_chunk(oc):
        load(q_hbm, q_ref, q_sem, oc).wait()
        grouped(oc, lambda o: intra(head_of(o)))

    is_second = core == 1
    is_after = side == 1

    def core_states(u):
        here, there = own_ref[u], s_recv[u].astype(F32)
        return jnp.where(is_second, there, here), jnp.where(is_second, here, there)

    def chip_state(u):
        early, late = core_states(u)
        return fade(mine(u), F32(rows), j_cores) * early + late

    def give_chip(w):
        a_send[w] = chip_state(w).astype(BF16)

    def keep_chip(w):
        chip_ref[w] = chip_state(quarter + w)

    def give_chunk(c):
        s_copy(c).wait_recv()
        grouped(c, give_chip)
        for i in range(step // few):
            a_copy(c * (step // few) + i).start()

    each(parts // 2, give_chunk)

    def keep_chunk(c):
        s_copy(parts // 2 + c).wait_recv()
        grouped(c, keep_chip)

    each(parts // 2, keep_chunk)

    def settle(u, enters):
        early, _ = core_states(u)
        second = fade(mine(u), F32(rows), j_enter) * enters + early
        carry_ref[u] = jnp.where(is_second, second, enters)
        c_send[u] = jnp.where(is_second, enters, second).astype(BF16)

    def chain(w):
        h = mine(quarter + w)
        here, there = chip_ref[w], a_recv[w].astype(F32)
        early, late = jnp.where(is_after, there, here), jnp.where(is_after, here, there)
        before = p_recv[w].astype(F32)
        total = fade(h, F32(2 * rows), j_chips) * early + late
        p_send[w] = (fade(h, F32(4 * rows), j_board) * before + total).astype(BF16)
        second = fade(h, F32(2 * rows), j_front) * before + early
        x_send[w] = jnp.where(is_after, before, second).astype(BF16)
        settle(quarter + w, jnp.where(is_after, second, before))

    def chain_chunk(c):
        a_copy(c).wait_recv()

        @pl.when(plane > 0)
        def _():
            p_copy(c).wait_recv()

        grouped(c, chain, few)

        @pl.when(plane < planes - 1)
        def _():
            p_copy(c).start()

        x_copy(c).start()
        c_copy(turns + c).start()

    def across_chunk(c):
        x_copy(c).wait_recv()
        grouped(c, lambda w: settle(w, x_recv[w].astype(F32)), few)
        c_copy(c).start()

    ready = jnp.minimum(2 + 2 * plane, chunks)
    each(ready, intra_chunk)
    each(turns, chain_chunk)
    each(chunks, intra_chunk, ready)
    each(turns, across_chunk)

    def finish_all(work):
        fades = [jnp.exp2(reach_ref[...] * rate(h)) for h, _ in work]
        states = [enters for _, enters in work]
        for b in range(blocks):
            here = pl.ds(b * BLOCK, BLOCK)
            squares = sq_ref[here, :]
            for i, (h, _) in enumerate(work):
                inter = jnp.dot(
                    q_ref[here, cols(h)], states[i].astype(BF16), preferred_element_type=F32
                )
                mixed = mixed_ref[here, cols(h)] + inter * (fades[i] * lead_ref[b])
                squares = squares + mixed * mixed
                out_ref[here, cols(h)] = mixed.astype(BF16)
                if b < blocks - 1:
                    states[i] = fade(h, F32(BLOCK), within[b]) * states[i] + local_ref[b, h]
            sq_ref[here, :] = squares

    def own_part(c):
        finish_all([(mine(c * step + i), carry_ref[c * step + i]) for i in range(step)])

    each(parts, own_part)

    def other_part(c):
        for i in range(step // few):
            c_copy(c * (step // few) + i).wait_recv()
        finish_all(
            [(theirs(c * step + i), c_recv[c * step + i].astype(F32)) for i in range(step)]
        )

    each(parts, other_part)

    ones = jnp.ones((8, size), F32)
    summed = lax.dot_general(
        ones, sq_ref[...], (((1,), (1,)), ((), ())),
        precision=lax.Precision.HIGHEST, preferred_element_type=F32,
    )
    sq_send[...] = summed

    def sq_copy(i):
        return pltpu.make_async_remote_copy(
            src_ref=sq_send, dst_ref=sq_recv.at[i], send_sem=sq_out.at[i], recv_sem=sq_in.at[i],
            device_id={"head": lax.rem(headpos + i, head_parts)}, device_id_type=MESH,
        )

    for i in range(1, head_parts):
        sq_copy(i).start()

    each(parts, lambda c: s_copy(c).wait_send())
    each(2 * turns, lambda c: c_copy(c).wait_send())

    def drain(c):
        a_copy(c).wait_send()
        x_copy(c).wait_send()

        @pl.when(plane < planes - 1)
        def _():
            p_copy(c).wait_send()

    each(turns, drain)
    for i in range(1, head_parts):
        sq_copy(i).wait_recv()
        summed = summed + sq_recv[i]
    inverse = lax.rsqrt(summed / F32(heads * size * head_parts) + F32(1e-05))
    inv_ref[...] = jnp.broadcast_to(jnp.transpose(inverse)[:, 0:1], inv_ref.shape)
    for i in range(1, head_parts):
        sq_copy(i).wait_send()


def scale_kernel(mixed_ref, inv_ref, gain_ref, final_hbm, final_ref, sem):
    rows, size = inv_ref.shape
    strip = rows // sem.shape[0]

    def move(i):
        here = pl.ds(i * strip, strip)
        return pltpu.make_async_copy(final_ref.at[here], final_hbm.at[here], sem.at[i])

    for i in range(sem.shape[0]):
        here = pl.ds(i * strip, strip)
        inverse = inv_ref[here, :]
        for c in range(0, final_ref.shape[1], size):
            piece = mixed_ref[here, c:c + size].astype(F32)
            final_ref[here, c:c + size] = (piece * inverse * gain_ref[:, c:c + size]).astype(BF16)
        move(i).start()
    for i in range(sem.shape[0]):
        move(i).wait()


def shards(planes, head_parts, queries, key_rows, values, slopes, doc_lengths, norm_gain):
    rows, feat = queries.shape
    heads = slopes.shape[0]
    size = feat // heads
    blocks = rows // BLOCK
    half = heads // 2
    quarter = half // 2
    step = min(4, quarter)
    few = max(1, quarter // 8)
    parts = half // step
    turns = quarter // few
    hbm = pl.BlockSpec(memory_space=pltpu.HBM)
    smem = pl.BlockSpec(memory_space=pltpu.SMEM)
    states = lambda count, dtype: pltpu.VMEM((count, size, size), dtype)
    dma = lambda n: pltpu.SemaphoreType.DMA((n,))
    mixed, inverse = pl.pallas_call(
        functools.partial(kernel, planes, head_parts, heads, blocks, step, few),
        out_shape=(
            jax.ShapeDtypeStruct((rows, feat), BF16),
            jax.ShapeDtypeStruct((rows, size), F32),
        ),
        in_specs=[smem, smem, hbm, hbm, hbm],
        out_specs=(pl.BlockSpec(memory_space=pltpu.VMEM), pl.BlockSpec(memory_space=pltpu.VMEM)),
        scratch_shapes=[
            pltpu.VMEM((rows, feat), BF16),
            pltpu.VMEM((rows, feat), BF16),
            pltpu.VMEM((rows, feat), BF16),
            pltpu.VMEM((rows, feat), F32),
            pltpu.VMEM((max(blocks - 1, 1), heads, size, size), F32),
            states(half, F32),
            states(half, F32),
            states(quarter, F32),
            *[states(half, BF16)] * 4,
            *[states(quarter, BF16)] * 6,
            pltpu.VMEM((BLOCK // 2, BLOCK), F32),
            pltpu.VMEM((blocks, BLOCK, BLOCK), F32),
            pltpu.VMEM((blocks, BLOCK, size), F32),
            pltpu.VMEM((blocks, BLOCK, size), F32),
            pltpu.VMEM((BLOCK, size), F32),
            pltpu.VMEM((BLOCK, size), F32),
            pltpu.VMEM((rows, size), F32),
            pltpu.VMEM((8, rows), F32),
            pltpu.VMEM((head_parts, 8, rows), F32),
            *[dma(2 * parts)] * 3,
            *[dma(parts)] * 2,
            *[dma(2 * turns)] * 2,
            *[dma(turns)] * 6,
            dma(head_parts),
            dma(head_parts),
        ],
        compiler_params=pltpu.CompilerParams(
            collective_id=0, has_side_effects=True, vmem_limit_bytes=47 * 1024 * 1024
        ),
    )(slopes, doc_lengths, queries, key_rows, values)
    vmem = pl.BlockSpec(memory_space=pltpu.VMEM)
    return pl.pallas_call(
        scale_kernel,
        out_shape=jax.ShapeDtypeStruct((rows, feat), BF16),
        in_specs=[vmem, vmem, vmem],
        out_specs=pl.BlockSpec(memory_space=pltpu.HBM),
        scratch_shapes=[pltpu.VMEM((rows, feat), BF16), pltpu.SemaphoreType.DMA((8,))],
        compiler_params=pltpu.CompilerParams(vmem_limit_bytes=9 * 1024 * 1024),
    )(mixed, inverse, norm_gain.reshape(1, feat))


def solution(mesh):
    placed = (P("seq", "head"), P("seq", "head"), P("seq", "head"), P("head"), P(), P("head"))
    return jax.shard_map(
        functools.partial(shards, mesh.shape["seq"] // 4, mesh.shape["head"]),
        mesh=mesh, in_specs=placed, out_specs=P("seq", "head"), check_vma=False,
    )
```
